128 devices in a mesh: seg: 8 (over x, core), row: 16 (over z, y).
Axes of the slice: x: 4, y: 4, z: 4, core: 2. Of those that a mesh axis runs over, the one named last changes fastest.
Arguments:
- wavefunction: bfloat16 [8192, 4, 1024], P(('seg', 'row')), may hold values from -110 to 110
- left_block: bfloat16 [8192, 1024], P(('seg', 'row')), may hold values from -2 to 2, as said below
- left_edge: bfloat16 [8192, 1024], P(('seg', 'row')), may hold values from -2 to 2, as said below
- right_block: bfloat16 [8192, 1024], P('seg'), may hold values from -2 to 2, as said below
- right_edge: bfloat16 [8192, 1024], P('seg'), may hold values from -2 to 2, as said below
- fields: float32 [8, 2], P('seg'), may hold values from 0.3 to 3
- bond_values: float32 [8, 1024], P('seg'), may hold values from 0.5 to 2
- kept_rank: int32 [8], P('seg'), may hold values from 512 to 1024
Outputs:
- updated_wave: bfloat16 [8192, 4, 1024], P(('seg', 'row'))
- joined_wave: bfloat16 [8192, 4, 1024], P(('seg', 'row'))
- energies: float32 [8], P('seg')
The draws below stay inside these ranges and needn't reach their ends.
Inputs may be any that keep to these rules, and one draw needn't show every extreme that they name: `left_block`: each segment's 1024 x 1024 block is symmetric. `left_edge`: each segment's 1024 x 1024 block is symmetric. `right_block`: each segment's 1024 x 1024 block is symmetric. `right_edge`: each segment's 1024 x 1024 block is symmetric.
All inputs are finite; a program needn't handle non-finite values.
Results may differ from the reference program's by a relative error of at most 0.006.
Values may be sent and summed in bfloat16 or wider, within the bound.
No kernel may reach another device: no remote copies, remote signals or barrier semaphores. Data moves between devices by JAX's collectives and lax.ppermute only.
A program may use at most 64 MiB of HBM per device.

```python
import math
import jax
import jax.numpy as jnp
from jax import lax

CHI = 1024
SEGS = 8


def symmetric_blocks(key, salt_value):
    inner = jax.random.fold_in(key, salt_value)
    entries = jnp.clip(jax.random.normal(inner, (SEGS, CHI, CHI), jnp.float32), -4.0, 4.0)
    symmetric = (entries + jnp.swapaxes(entries, 1, 2)) / jnp.sqrt(2.0 * CHI)
    return symmetric.reshape(SEGS * CHI, CHI)


def draw_left_block(key, part):
    return symmetric_blocks(key, 11).astype(jnp.bfloat16)


def draw_left_edge(key, part):
    return symmetric_blocks(key, 23).astype(jnp.bfloat16)


def draw_right_block(key, part):
    return symmetric_blocks(key, 37).astype(jnp.bfloat16)


def draw_right_edge(key, part):
    return symmetric_blocks(key, 41).astype(jnp.bfloat16)


def draw_wavefunction(key, part):
    inner = jax.random.fold_in(key, 5)
    key_one, key_two, key_three = jax.random.split(inner, 3)
    entries = jnp.clip(jax.random.normal(key_one, (SEGS, CHI, 4, CHI), jnp.float32), -4.0, 4.0)
    log_top = math.log(10.0)
    ramp = jnp.exp2(jnp.arange(CHI, dtype=jnp.float32) / CHI).reshape(1, CHI, 1, 1)
    row_scale = jnp.exp(jax.random.uniform(key_two, (SEGS, CHI, 1, 1), jnp.float32) * log_top) * ramp
    col_scale = jnp.exp(jax.random.uniform(key_three, (SEGS, 1, 1, CHI), jnp.float32) * log_top)
    return (entries * row_scale * col_scale / 8.0).reshape(SEGS * CHI, 4, CHI).astype(jnp.bfloat16)


def with_ends(result, own_key, least, high):
    extent = result.shape
    place = [jax.random.randint(jax.random.fold_in(own_key, axis), (), 0, extent[axis]) for axis in range(len(extent))]
    result = result.at[tuple(place)].set(least)
    longest = extent.index(max(extent))
    place[longest] = (place[longest] + 1) % extent[longest]
    return result.at[tuple(place)].set(high)


def steps_of(own_key, dims, shards, smallest, high):
    gain, own = 1.0, jax.random.fold_in(own_key, 6)
    for position, parts in shards:
        heights = jnp.exp(jax.random.uniform(jax.random.fold_in(own, position), (parts,), jnp.float32, smallest / len(shards), high / len(shards)))
        gain = gain * jnp.repeat(heights, dims[position] // parts).reshape([-1 if axis == position else 1 for axis in range(len(dims))])
    return gain


def setup_inputs(seed: int = 0) -> dict:
    splits = jax.random.split(jax.random.key(seed), 9)
    wavefunction = draw_wavefunction(jax.random.fold_in(splits[8], 71), 0)
    left_block = draw_left_block(jax.random.fold_in(splits[8], 71), 0)
    left_edge = draw_left_edge(jax.random.fold_in(splits[8], 71), 0)
    right_block = draw_right_block(jax.random.fold_in(splits[8], 71), 0)
    right_edge = draw_right_edge(jax.random.fold_in(splits[8], 71), 0)
    fields = jnp.clip(jnp.exp(math.log(3.0) - 2.3025851 * jax.random.uniform(splits[5], (SEGS, 2), jnp.float32) ** steps_of(splits[5], (SEGS, 2), ((0, 8),), -0.2, 0.2)), 0.3, 3.0)
    bond_values = jnp.clip(jnp.exp(math.log(2.0) - 1.3862944 * jax.random.uniform(splits[6], (SEGS, CHI), jnp.float32) ** steps_of(splits[6], (SEGS, CHI), ((0, 8),), -0.2, 0.2)), 0.5, 2.0)
    kept_rank = with_ends(jax.random.randint(splits[7], (SEGS,), CHI // 2, CHI + 1), jax.random.fold_in(splits[7], 1), CHI // 2, CHI).astype(jnp.int32)
    return dict(wavefunction=wavefunction, left_block=left_block, left_edge=left_edge, right_block=right_block, right_edge=right_edge, fields=fields, bond_values=bond_values, kept_rank=kept_rank)


STEP_SIZE = 0.25

def apply_segment(psi_block, block_h, edge_h, block_r, edge_r, field_pair):
    flattened = psi_block.reshape(CHI, 4 * CHI)
    left_h = jnp.dot(block_h, flattened, preferred_element_type=jnp.float32).reshape(CHI, 4, CHI)
    left_z = jnp.dot(edge_h, flattened, preferred_element_type=jnp.float32).reshape(CHI, 4, CHI)
    columns = psi_block.reshape(CHI * 4, CHI)
    right_h = jnp.dot(columns, block_r, preferred_element_type=jnp.float32).reshape(CHI, 4, CHI)
    right_z = jnp.dot(columns, edge_r, preferred_element_type=jnp.float32).reshape(CHI, 4, CHI)
    sign_one = jnp.array([1.0, 1.0, -1.0, -1.0], jnp.float32).reshape(1, 4, 1)
    sign_two = jnp.array([1.0, -1.0, 1.0, -1.0], jnp.float32).reshape(1, 4, 1)
    values = psi_block.astype(jnp.float32)
    swap_one = jnp.concatenate([values[:, 2:4], values[:, 0:2]], 1)
    swap_two = jnp.stack([values[:, 1], values[:, 0], values[:, 3], values[:, 2]], 1)
    applied = left_h + sign_one * left_z + right_h + sign_two * right_z - sign_one * sign_two * values - field_pair[0] * swap_one - field_pair[1] * swap_two
    squares = jnp.sum(values * values)
    rayleigh = jnp.sum(values * applied)
    energy = rayleigh / squares
    stepped = values - STEP_SIZE * (applied - energy * values)
    renorm = jnp.sum(stepped * stepped)
    renewed = (stepped * jnp.sqrt(CHI / renorm)).astype(jnp.bfloat16)
    return (renewed, energy)

def reference(wavefunction, left_block, left_edge, right_block, right_edge, fields, bond_values, kept_rank):
    waves = wavefunction.reshape(SEGS, CHI, 4, CHI)
    blocks_l = left_block.reshape(SEGS, CHI, CHI)
    edges_l = left_edge.reshape(SEGS, CHI, CHI)
    blocks_r = right_block.reshape(SEGS, CHI, CHI)
    edges_r = right_edge.reshape(SEGS, CHI, CHI)

    def update(operands):
        return apply_segment(*operands)
    renewed, energies = lax.map(update, (waves, blocks_l, edges_l, blocks_r, edges_r, fields))

    def weigh(operands):
        wave_new, singular, kept_count = operands
        columns = wave_new.reshape(CHI * 4, CHI)
        gram = jnp.dot(columns.T, columns, preferred_element_type=jnp.float32)
        positions = jnp.arange(CHI)
        inverse = jnp.where(positions < kept_count, 1.0 / singular, 0.0)
        return (inverse[:, None] * gram * inverse[None, :]).astype(jnp.bfloat16)
    weights = lax.map(weigh, (renewed, bond_values, kept_rank))
    preceding = jnp.concatenate([jnp.zeros((1, CHI, CHI), weights.dtype), weights[:-1]], 0)

    def join(operands):
        earlier, wave_new = operands
        product = jnp.dot(earlier, wave_new.reshape(CHI, 4 * CHI), preferred_element_type=jnp.float32)
        return product.astype(jnp.bfloat16).reshape(CHI, 4, CHI)
    joined = lax.map(join, (preceding, renewed))
    return (renewed.reshape(SEGS * CHI, 4, CHI), joined.reshape(SEGS * CHI, 4, CHI), energies)
```

```python
import jax
import jax.numpy as jnp
from jax import lax
from jax.experimental import pallas as pl
from jax.experimental.pallas import tpu as pltpu
from jax.sharding import PartitionSpec as P

STEP_SIZE = 0.25

SIDE = 4
F32 = jnp.float32
BF16 = jnp.bfloat16


def place():
    row = lax.axis_index("row")
    return row // SIDE, row % SIDE


def along_y(value, step):
    pairs = [
        (z * SIDE + y, z * SIDE + (y + step) % SIDE) for z in range(SIDE) for y in range(SIDE)
    ]
    return lax.ppermute(value, "row", pairs)


def along_z(value, step):
    pairs = [
        (z * SIDE + y, ((z + step) % SIDE) * SIDE + y) for z in range(SIDE) for y in range(SIDE)
    ]
    return lax.ppermute(value, "row", pairs)


def to_next_segment(value, step):
    count = lax.axis_size("seg")
    side = SIDE * SIDE
    pairs = [
        (k * side + z * SIDE + y, (k + 1) * side + z * SIDE + (y + step) % SIDE)
        for k in range(count - 1)
        for z in range(SIDE)
        for y in range(SIDE)
    ]
    return lax.ppermute(value, ("seg", "row"), pairs)


def cost(flops, moved):
    return pl.CostEstimate(flops=flops, bytes_accessed=moved, transcendentals=0)


def call(kernel, outs, args, flops, scratch=(), smem=()):
    moved = sum(a.size * a.dtype.itemsize for a in args)
    moved += sum(o.size * o.dtype.itemsize for o in outs)
    specs = [
        pl.BlockSpec(memory_space=pltpu.SMEM if i in smem else pltpu.VMEM)
        for i in range(len(args))
    ]
    return pl.pallas_call(
        kernel,
        out_shape=tuple(outs),
        in_specs=specs,
        out_specs=tuple(pl.BlockSpec(memory_space=pltpu.VMEM) for _ in outs),
        scratch_shapes=list(scratch),
        cost_estimate=cost(flops, moved),
    )(*args)


def shape(dims, dtype):
    return jax.ShapeDtypeStruct(dims, dtype)


def rows_at(index, count):
    return pl.ds(pl.multiple_of(index * count, count), count)


def dot(a, b):
    return jnp.dot(a, b, preferred_element_type=F32)


def assemble_kernel(own_ref, p1, p2, p3, out_ref):
    _, y = place()
    count = p1.shape[0]
    out_ref[rows_at(y, count), :] = own_ref[y]
    for step, ref in ((1, p1), (2, p2), (3, p3)):
        out_ref[rows_at((y - step) % SIDE, count), :] = ref[...]


def right_kernel(fields_ref, block_ref, rh_ref, rz_ref, own_ref, q1, q2, q3, out_ref):
    _, y = place()
    count = own_ref.shape[1]
    sign_one = (1 - 2 * (y // 2)).astype(F32)
    sign_two = (1 - 2 * (y % 2)).astype(F32)
    field_one, field_two = fields_ref[0, 0], fields_ref[0, 1]
    block = block_ref[...]
    values = block.astype(F32)
    total = dot(block, rh_ref[...]) + sign_two * dot(block, rz_ref[...])
    out_ref[...] = total - (sign_one * sign_two) * values

    def subtract(at, flip_two, flip_one):
        rows = rows_at(at, count)
        out_ref[rows, :] = (
            out_ref[rows, :] - field_one * flip_one.astype(F32) - field_two * flip_two.astype(F32)
        )

    subtract(y, own_ref[y ^ 1], own_ref[y ^ 2])
    for step, ref in ((1, q1), (2, q2), (3, q3)):
        subtract((y - step) % SIDE, ref[0], ref[1])


def left_kernel(
    right_ref, block_ref, g1, g2, g3, lh_ref, lz_ref, q1, q2, q3, image_ref, stats_ref, lefts
):
    row = lax.axis_index("row")
    z, y = place()
    count = lh_ref.shape[0]
    depth = block_ref.shape[0]
    sign_one = (1 - 2 * (y // 2)).astype(F32)

    def put(at, left, edge):
        rows = rows_at(at, count)
        lefts[0, rows, :] = left
        lefts[1, rows, :] = (edge.astype(F32) * sign_one).astype(BF16)

    put(y, lh_ref[...], lz_ref[...])
    for step, ref in ((1, q1), (2, q2), (3, q3)):
        put((y - step) % SIDE, ref[2], ref[3])
    applied = right_ref[...]
    for step, ref in ((0, block_ref), (1, g1), (3, g3), (2, g2)):
        columns = rows_at((z - step) % SIDE, depth)
        block = ref[...]
        applied += dot(lefts[0, :, columns], block) + dot(lefts[1, :, columns], block)
    values = block_ref[...].astype(F32)
    squares = jnp.sum(values * values)
    rayleigh = jnp.sum(values * applied)
    quotient = jnp.where(squares > 0.0, rayleigh / squares, 0.0)
    image = applied - quotient * values
    image_ref[...] = image.astype(BF16)
    spread = jnp.sum(image * image)
    cross = jnp.sum(image * values)
    lane = lax.broadcasted_iota(jnp.int32, stats_ref.shape, 1)
    mine = lax.broadcasted_iota(jnp.int32, stats_ref.shape, 0) == row
    stats = jnp.zeros(stats_ref.shape, F32)
    for i, item in enumerate((squares, rayleigh, spread, cross, quotient)):
        stats = jnp.where(mine & (lane == i), item, stats)
    stats_ref[...] = stats


def scalars_kernel(bond_dim, stats_ref, coef_ref):
    stats = stats_ref[...]
    squares, rayleigh, spread, cross, quotient = (stats[:, i : i + 1] for i in range(5))
    all_squares = jnp.sum(squares, axis=0, keepdims=True)
    energy = jnp.sum(rayleigh, axis=0, keepdims=True) / all_squares
    shift = quotient - energy
    distance = jnp.sum(spread + 2.0 * shift * cross + shift * shift * squares, axis=0, keepdims=True)
    renorm = all_squares + STEP_SIZE * STEP_SIZE * distance
    scale = jnp.sqrt(bond_dim / renorm)
    lane = lax.broadcasted_iota(jnp.int32, coef_ref.shape, 1)
    coef = jnp.where(lane == 0, scale * (1.0 - STEP_SIZE * shift), 0.0)
    coef = jnp.where(lane == 1, -STEP_SIZE * scale, coef)
    coef_ref[...] = jnp.where(lane == 2, energy, coef)


def gram_kernel(coef_ref, b0, b1, b2, b3, a0, a1, a2, a3, wave_ref, o0, o1, o2, o3, total):
    z, y = place()
    depth = b0.shape[0]
    count = o0.shape[0]
    for step, block, image in ((0, b0, a0), (1, b1, a1), (3, b3, a3), (2, b2, a2)):
        from_z = (z - step) % SIDE
        index = from_z * SIDE + y
        wave_ref[rows_at(from_z, depth), :] = (
            coef_ref[index, 0] * block[...].astype(F32)
            + coef_ref[index, 1] * image[...].astype(F32)
        ).astype(BF16)
    mine = wave_ref[:, rows_at(z, depth)]
    total[...] = lax.dot_general(
        mine, wave_ref[...], (((0,), (0,)), ((), ())), preferred_element_type=F32
    )
    for step, out in ((0, o0), (1, o1), (2, o2), (3, o3)):
        out[...] = total[rows_at((y + step) % SIDE, count), :]


def weigh_kernel(p0, p1, p2, p3, rows_ref, columns_ref, out_ref):
    gram = p0[...] + p1[...] + p2[...] + p3[...]
    out_ref[...] = (rows_ref[:, :1] * gram * columns_ref[...]).astype(BF16)


def join_kernel(w0, w1, w2, w3, wave_ref, o0, o1, o2, o3, weights):
    count = w0.shape[0]
    for i, ref in enumerate((w0, w1, w2, w3)):
        weights[i * count : (i + 1) * count, :] = ref[...]
    product = dot(weights[...], wave_ref[...]).astype(BF16)
    for i, out in enumerate((o0, o1, o2, o3)):
        out[...] = product[i * count : (i + 1) * count, :]


def body(
    wavefunction, left_block, left_edge, right_block, right_edge, fields, bond_values, kept_rank
):
    count, _, bond = wavefunction.shape
    depth = SIDE * count
    z, y = place()
    spins = jnp.moveaxis(wavefunction, 1, 0)

    def spin(index):
        return lax.dynamic_index_in_dim(spins, index, 0, keepdims=False)

    early = [along_y(spin((y + s) % SIDE), s) for s in (1, 2, 3)]
    (block,) = call(assemble_kernel, [shape((depth, bond), BF16)], [spins, *early], 0)
    g1, g3, g2 = (along_z(block, s) for s in (1, 3, 2))

    def bundle(s):
        target = (y + s) % SIDE
        return jnp.stack([spin(target ^ 1), spin(target ^ 2), left_block, left_edge])

    q1, q2, q3 = (along_y(bundle(s), s) for s in (1, 2, 3))
    (right,) = call(
        right_kernel,
        [shape((depth, bond), F32)],
        [fields, block, right_block, right_edge, spins, q1, q2, q3],
        4 * depth * bond * bond,
        smem=(0,),
    )
    image, stats = call(
        left_kernel,
        [shape((depth, bond), BF16), shape((SIDE * SIDE, 128), F32)],
        [right, block, g1, g2, g3, left_block, left_edge, q1, q2, q3],
        4 * depth * bond * bond,
        scratch=[pltpu.VMEM((2, depth, bond), BF16)],
    )
    a1, a3, a2 = (along_z(image, s) for s in (1, 3, 2))
    stats = stats + along_y(stats, 1) + along_y(stats, 2) + along_y(stats, 3)
    stats = stats + along_z(stats, 1) + along_z(stats, 2) + along_z(stats, 3)
    (coef,) = call(
        lambda s, c: scalars_kernel(bond, s, c), [shape(stats.shape, F32)], [stats], 0
    )
    energy = coef[0, 2]

    image_rows = image.reshape(SIDE, count, bond)

    def own_image(s):
        return lax.dynamic_index_in_dim(image_rows, (y + s) % SIDE, 0, keepdims=False)

    pieces = [own_image(0)] + [along_y(own_image(s), s) for s in (1, 2, 3)]
    ordered = jnp.stack([pieces[0], pieces[3], pieces[2], pieces[1]])
    images = jnp.roll(ordered, y, 0)
    mine = lax.dynamic_slice_in_dim(coef, z * SIDE, SIDE, 0)
    wave_rows = (
        mine[:, 0].reshape(SIDE, 1, 1) * spins.astype(F32)
        + mine[:, 1].reshape(SIDE, 1, 1) * images.astype(F32)
    ).astype(BF16)
    wave_new = jnp.moveaxis(wave_rows, 0, 1)

    wave, *partial = call(
        gram_kernel,
        [shape((SIDE * depth, bond), BF16)] + [shape((count, bond), F32)] * SIDE,
        [coef, block, g1, g2, g3, image, a1, a2, a3],
        2 * depth * bond * bond,
        scratch=[pltpu.VMEM((depth, bond), F32)],
        smem=(0,),
    )
    parts = [partial[0]] + [along_y(partial[s], s) for s in (1, 2, 3)]
    positions = jnp.arange(bond)
    inverse = jnp.where(positions < kept_rank[0], 1.0 / bond_values[0], 0.0)
    inverse_rows = lax.dynamic_slice_in_dim(inverse, (z * SIDE + y) * count, count, 0)
    (weighted,) = call(
        weigh_kernel,
        [shape((count, bond), BF16)],
        [
            *parts,
            jnp.broadcast_to(inverse_rows[:, None], (count, 128)),
            inverse.reshape(1, bond),
        ],
        0,
    )
    previous = [to_next_segment(weighted, s) for s in (0, 1, 2, 3)]
    joined = call(
        join_kernel,
        [shape((count, bond), BF16)] * SIDE,
        [*previous, wave],
        2 * depth * bond * bond,
        scratch=[pltpu.VMEM((depth, bond), BF16)],
    )
    back = [joined[0]] + [along_y(joined[s], -s) for s in (1, 2, 3)]
    joined_wave = jnp.moveaxis(jnp.roll(jnp.stack(back), y, 0), 0, 1)
    return (wave_new, joined_wave, energy.reshape(1))


def solution(mesh):
    in_specs = (
        P(("seg", "row"), None, None),
        P(("seg", "row"), None),
        P(("seg", "row"), None),
        P("seg", None),
        P("seg", None),
        P("seg", None),
        P("seg", None),
        P("seg"),
    )
    out_specs = (P(("seg", "row"), None, None), P(("seg", "row"), None, None), P("seg"))
    return jax.shard_map(body, mesh=mesh, in_specs=in_specs, out_specs=out_specs, check_vma=False)
```

```python
import jax
import jax.numpy as jnp
from jax import lax
from jax.experimental import pallas as pl
from jax.experimental.pallas import tpu as pltpu
from jax.sharding import PartitionSpec as P

STEP_SIZE = 0.25

SIDE = 4
F32 = jnp.float32
BF16 = jnp.bfloat16


def place():
    row = lax.axis_index("row")
    odd = lax.axis_index("seg") % 2 == 1
    z, y = row // SIDE, row % SIDE
    return jnp.where(odd, y, z), jnp.where(odd, z, y)


def row_of(group, spin):
    odd = lax.axis_index("seg") % 2 == 1
    return jnp.where(odd, spin * SIDE + group, group * SIDE + spin)


def moved(row, step, on_z):
    z, y = row // SIDE, row % SIDE
    return ((z + step) % SIDE) * SIDE + y if on_z else z * SIDE + (y + step) % SIDE


def along(value, step, over_group):
    rows = SIDE * SIDE
    pairs = [
        (k * rows + row, k * rows + moved(row, step, over_group == (k % 2 == 0)))
        for k in range(lax.axis_size("seg"))
        for row in range(rows)
    ]
    return lax.ppermute(value, ("seg", "row"), pairs)


def along_spin(value, step):
    return along(value, step, False)


def along_group(value, step):
    return along(value, step, True)


def to_next_segment(value, step):
    rows = SIDE * SIDE
    pairs = [
        (k * rows + row, (k + 1) * rows + moved(row, step, (k + 1) % 2 == 1))
        for k in range(lax.axis_size("seg") - 1)
        for row in range(rows)
    ]
    return lax.ppermute(value, ("seg", "row"), pairs)


def cost(flops, moved):
    return pl.CostEstimate(flops=flops, bytes_accessed=moved, transcendentals=0)


def call(kernel, outs, args, flops, scratch=(), smem=()):
    moved = sum(a.size * a.dtype.itemsize for a in args)
    moved += sum(o.size * o.dtype.itemsize for o in outs)
    specs = [
        pl.BlockSpec(memory_space=pltpu.SMEM if i in smem else pltpu.VMEM)
        for i in range(len(args))
    ]
    return pl.pallas_call(
        kernel,
        out_shape=tuple(outs),
        in_specs=specs,
        out_specs=tuple(pl.BlockSpec(memory_space=pltpu.VMEM) for _ in outs),
        scratch_shapes=list(scratch),
        cost_estimate=cost(flops, moved),
    )(*args)


def shape(dims, dtype):
    return jax.ShapeDtypeStruct(dims, dtype)


def rows_at(index, count):
    return pl.ds(pl.multiple_of(index * count, count), count)


def dot(a, b):
    return jnp.dot(a, b, preferred_element_type=F32)


def assemble_kernel(own_ref, p1, p2, p3, out_ref):
    _, spin = place()
    count = p1.shape[0]
    out_ref[rows_at(spin, count), :] = own_ref[spin]
    for step, ref in ((1, p1), (2, p2), (3, p3)):
        out_ref[rows_at((spin - step) % SIDE, count), :] = ref[...]


def right_kernel(block_ref, rh_ref, rz_ref, out_ref):
    _, spin = place()
    sign_one = (1 - 2 * (spin // 2)).astype(F32)
    sign_two = (1 - 2 * (spin % 2)).astype(F32)
    block = block_ref[...]
    total = dot(block, rh_ref[...]) + sign_two * dot(block, rz_ref[...])
    out_ref[...] = total - (sign_one * sign_two) * block.astype(F32)


def left_kernel(
    fields_ref,
    right_ref,
    block_ref,
    g1,
    g2,
    g3,
    own_ref,
    lh_ref,
    lz_ref,
    q1,
    q2,
    q3,
    image_ref,
    stats_ref,
    lefts,
    psi,
    applied_ref,
):
    row = lax.axis_index("row")
    group, spin = place()
    count = lh_ref.shape[0]
    sign_one = (1 - 2 * (spin // 2)).astype(F32)
    field_one, field_two = fields_ref[0, 0], fields_ref[0, 1]

    def put(at, flip_two, flip_one, left, edge):
        rows = rows_at(at, count)
        lefts[0, rows, :] = left
        lefts[1, rows, :] = (edge.astype(F32) * sign_one).astype(BF16)
        applied_ref[rows, :] = (
            right_ref[rows, :] - field_one * flip_one.astype(F32) - field_two * flip_two.astype(F32)
        )

    put(spin, own_ref[spin ^ 1], own_ref[spin ^ 2], lh_ref[...], lz_ref[...])
    for step, ref in ((1, q1), (2, q2), (3, q3)):
        put((spin - step) % SIDE, ref[0], ref[1], ref[2], ref[3])
    for step, ref in ((0, block_ref), (1, g1), (3, g3), (2, g2)):
        for i in range(SIDE):
            at = row_of((group - step) % SIDE, i)
            psi[rows_at(at, count), :] = ref[i * count : (i + 1) * count, :]
    applied = applied_ref[...] + dot(lefts[0], psi[...]) + dot(lefts[1], psi[...])
    values = block_ref[...].astype(F32)
    squares = jnp.sum(values * values)
    rayleigh = jnp.sum(values * applied)
    quotient = jnp.where(squares > 0.0, rayleigh / squares, 0.0)
    image = applied - quotient * values
    image_ref[...] = image.astype(BF16)
    spread = jnp.sum(image * image)
    cross = jnp.sum(image * values)
    lane = lax.broadcasted_iota(jnp.int32, stats_ref.shape, 1)
    mine = lax.broadcasted_iota(jnp.int32, stats_ref.shape, 0) == row
    stats = jnp.zeros(stats_ref.shape, F32)
    for i, item in enumerate((squares, rayleigh, spread, cross, quotient)):
        stats = jnp.where(mine & (lane == i), item, stats)
    stats_ref[...] = stats


def scalars_kernel(bond_dim, stats_ref, coef_ref):
    stats = stats_ref[...]
    squares, rayleigh, spread, cross, quotient = (stats[:, i : i + 1] for i in range(5))
    all_squares = jnp.sum(squares, axis=0, keepdims=True)
    energy = jnp.sum(rayleigh, axis=0, keepdims=True) / all_squares
    shift = quotient - energy
    distance = jnp.sum(spread + 2.0 * shift * cross + shift * shift * squares, axis=0, keepdims=True)
    renorm = all_squares + STEP_SIZE * STEP_SIZE * distance
    scale = jnp.sqrt(bond_dim / renorm)
    lane = lax.broadcasted_iota(jnp.int32, coef_ref.shape, 1)
    coef = jnp.where(lane == 0, scale * (1.0 - STEP_SIZE * shift), 0.0)
    coef = jnp.where(lane == 1, -STEP_SIZE * scale, coef)
    coef_ref[...] = jnp.where(lane == 2, energy, coef)


def gram_kernel(coef_ref, b0, b1, b2, b3, a0, a1, a2, a3, wave_ref, o0, o1, o2, o3, total):
    group, spin = place()
    count = o0.shape[0]
    for step, block, image in ((0, b0, a0), (1, b1, a1), (3, b3, a3), (2, b2, a2)):
        from_group = (group - step) % SIDE
        index = row_of(from_group, spin)
        for i in range(SIDE):
            rows = slice(i * count, (i + 1) * count)
            wave_ref[rows_at(row_of(from_group, i), count), :] = (
                coef_ref[index, 0] * block[rows, :].astype(F32)
                + coef_ref[index, 1] * image[rows, :].astype(F32)
            ).astype(BF16)
    for step, out in ((0, o0), (1, o1), (2, o2), (3, o3)):
        at = row_of(group, (spin + step) % SIDE)
        pair = wave_ref[:, rows_at(at // 2, 2 * count)]
        total[...] = lax.dot_general(
            pair, wave_ref[...], (((0,), (0,)), ((), ())), preferred_element_type=F32
        )
        out[...] = total[rows_at(at % 2, count), :]


def weigh_kernel(p0, p1, p2, p3, rows_ref, columns_ref, out_ref):
    gram = p0[...] + p1[...] + p2[...] + p3[...]
    out_ref[...] = (rows_ref[:, :1] * gram * columns_ref[...]).astype(BF16)


def join_kernel(w0, w1, w2, w3, wave_ref, o0, o1, o2, o3, weights):
    count = w0.shape[0]
    for i, ref in enumerate((w0, w1, w2, w3)):
        weights[i * count : (i + 1) * count, :] = ref[...]
    product = dot(weights[...], wave_ref[...]).astype(BF16)
    for i, out in enumerate((o0, o1, o2, o3)):
        out[...] = product[i * count : (i + 1) * count, :]


def body(
    wavefunction, left_block, left_edge, right_block, right_edge, fields, bond_values, kept_rank
):
    count, _, bond = wavefunction.shape
    depth = SIDE * count
    row = lax.axis_index("row")
    group, spin = place()
    odd = lax.axis_index("seg") % 2 == 1
    spins = jnp.moveaxis(wavefunction, 1, 0)

    def rows_of_spin(index):
        return lax.dynamic_index_in_dim(spins, index, 0, keepdims=False)

    early = [along_spin(rows_of_spin((spin + s) % SIDE), s) for s in (1, 2, 3)]
    (block,) = call(assemble_kernel, [shape((depth, bond), BF16)], [spins, *early], 0)
    g1, g3, g2 = (along_group(block, s) for s in (1, 3, 2))

    def bundle(s):
        target = (spin + s) % SIDE
        return jnp.stack(
            [rows_of_spin(target ^ 1), rows_of_spin(target ^ 2), left_block, left_edge]
        )

    q1, q2, q3 = (along_spin(bundle(s), s) for s in (1, 2, 3))
    (right,) = call(
        right_kernel,
        [shape((depth, bond), F32)],
        [block, right_block, right_edge],
        4 * depth * bond * bond,
    )
    image, stats = call(
        left_kernel,
        [shape((depth, bond), BF16), shape((SIDE * SIDE, 128), F32)],
        [fields, right, block, g1, g2, g3, spins, left_block, left_edge, q1, q2, q3],
        4 * depth * bond * bond,
        scratch=[
            pltpu.VMEM((2, depth, bond), BF16),
            pltpu.VMEM((SIDE * depth, bond), BF16),
            pltpu.VMEM((depth, bond), F32),
        ],
        smem=(0,),
    )
    a1, a3, a2 = (along_group(image, s) for s in (1, 3, 2))
    for hop in (along_spin, along_group):
        stats = stats + hop(stats, 1) + hop(stats, 2) + hop(stats, 3)
    (coef,) = call(
        lambda s, c: scalars_kernel(bond, s, c), [shape(stats.shape, F32)], [stats], 0
    )
    energy = coef[0, 2]

    image_rows = image.reshape(SIDE, count, bond)

    def rows_of_member(index):
        return lax.dynamic_index_in_dim(image_rows, index, 0, keepdims=False)

    pieces = [rows_of_member(spin)]
    pieces += [along_spin(rows_of_member((spin + s) % SIDE), s) for s in (1, 2, 3)]
    images = jnp.roll(jnp.stack([pieces[0], pieces[3], pieces[2], pieces[1]]), spin, 0)
    square = coef.reshape(SIDE, SIDE, -1)
    mine = jnp.where(
        odd,
        lax.dynamic_index_in_dim(square, group, 1, keepdims=False),
        lax.dynamic_index_in_dim(square, group, 0, keepdims=False),
    )
    wave_rows = (
        mine[:, 0].reshape(SIDE, 1, 1) * spins.astype(F32)
        + mine[:, 1].reshape(SIDE, 1, 1) * images.astype(F32)
    ).astype(BF16)
    wave_new = jnp.moveaxis(wave_rows, 0, 1)

    wave, *partial = call(
        gram_kernel,
        [shape((SIDE * depth, bond), BF16)] + [shape((count, bond), F32)] * SIDE,
        [coef, block, g1, g2, g3, image, a1, a2, a3],
        4 * depth * bond * bond,
        scratch=[pltpu.VMEM((2 * count, bond), F32)],
        smem=(0,),
    )
    parts = [partial[0]] + [along_spin(partial[s], s) for s in (1, 2, 3)]
    positions = jnp.arange(bond)
    inverse = jnp.where(positions < kept_rank[0], 1.0 / bond_values[0], 0.0)
    inverse_rows = lax.dynamic_slice_in_dim(inverse, row * count, count, 0)
    (weighted,) = call(
        weigh_kernel,
        [shape((count, bond), BF16)],
        [
            *parts,
            jnp.broadcast_to(inverse_rows[:, None], (count, 128)),
            inverse.reshape(1, bond),
        ],
        0,
    )
    previous = [to_next_segment(weighted, s) for s in (0, 1, 2, 3)]
    joined = call(
        join_kernel,
        [shape((count, bond), BF16)] * SIDE,
        [*previous, wave],
        2 * depth * bond * bond,
        scratch=[pltpu.VMEM((depth, bond), BF16)],
    )
    back = [joined[0]] + [along_spin(joined[s], -s) for s in (1, 2, 3)]
    joined_wave = jnp.moveaxis(jnp.roll(jnp.stack(back), spin, 0), 0, 1)
    return (wave_new, joined_wave, energy.reshape(1))


def solution(mesh):
    in_specs = (
        P(("seg", "row"), None, None),
        P(("seg", "row"), None),
        P(("seg", "row"), None),
        P("seg", None),
        P("seg", None),
        P("seg", None),
        P("seg", None),
        P("seg"),
    )
    out_specs = (P(("seg", "row"), None, None), P(("seg", "row"), None, None), P("seg"))
    return jax.shard_map(body, mesh=mesh, in_specs=in_specs, out_specs=out_specs, check_vma=False)
```

```python
import jax
import jax.numpy as jnp
from jax import lax
from jax.experimental import pallas as pl
from jax.experimental.pallas import tpu as pltpu
from jax.sharding import PartitionSpec as P

STEP_SIZE = 0.25

SIDE = 4
F32 = jnp.float32
BF16 = jnp.bfloat16


def place():
    row = lax.axis_index("row")
    odd = lax.axis_index("seg") % 2 == 1
    z, y = row // SIDE, row % SIDE
    return jnp.where(odd, y, z), jnp.where(odd, z, y)


def row_of(group, spin):
    odd = lax.axis_index("seg") % 2 == 1
    return jnp.where(odd, spin * SIDE + group, group * SIDE + spin)


def moved(row, step, on_z):
    z, y = row // SIDE, row % SIDE
    return ((z + step) % SIDE) * SIDE + y if on_z else z * SIDE + (y + step) % SIDE


def along(value, step, over_group):
    rows = SIDE * SIDE
    pairs = [
        (k * rows + row, k * rows + moved(row, step, over_group == (k % 2 == 0)))
        for k in range(lax.axis_size("seg"))
        for row in range(rows)
    ]
    return lax.ppermute(value, ("seg", "row"), pairs)


def along_spin(value, step):
    return along(value, step, False)


def along_group(value, step):
    return along(value, step, True)


def to_next_segment(value):
    return lax.ppermute(value, "seg", [(k, k + 1) for k in range(lax.axis_size("seg") - 1)])


def cost(flops, moved):
    return pl.CostEstimate(flops=flops, bytes_accessed=moved, transcendentals=0)


def call(kernel, outs, args, flops, scratch=(), smem=(), far=()):
    moved_bytes = sum(a.size * a.dtype.itemsize for a in args)
    moved_bytes += sum(o.size * o.dtype.itemsize for o in outs)

    def space(i):
        return pltpu.SMEM if i in smem else pl.ANY if i in far else pltpu.VMEM

    return pl.pallas_call(
        kernel,
        out_shape=tuple(outs),
        in_specs=[pl.BlockSpec(memory_space=space(i)) for i in range(len(args))],
        out_specs=tuple(pl.BlockSpec(memory_space=pltpu.VMEM) for _ in outs),
        scratch_shapes=list(scratch),
        cost_estimate=cost(flops, moved_bytes),
    )(*args)


def shape(dims, dtype):
    return jax.ShapeDtypeStruct(dims, dtype)


def rows_at(index, count):
    return pl.ds(pl.multiple_of(index * count, count), count)


def dot(a, b):
    return jnp.dot(a, b, preferred_element_type=F32)


def assemble_kernel(own_ref, p1, p2, p3, out_ref):
    _, spin = place()
    count = p1.shape[0]
    out_ref[rows_at(spin, count), :] = own_ref[spin]
    for step, ref in ((1, p1), (2, p2), (3, p3)):
        out_ref[rows_at((spin - step) % SIDE, count), :] = ref[...]


def right_kernel(block_ref, rh_ref, rz_ref, out_ref):
    _, spin = place()
    sign_one = (1 - 2 * (spin // 2)).astype(F32)
    sign_two = (1 - 2 * (spin % 2)).astype(F32)
    block = block_ref[...]
    total = dot(block, rh_ref[...]) + sign_two * dot(block, rz_ref[...])
    out_ref[...] = total - (sign_one * sign_two) * block.astype(F32)


def left_kernel(
    fields_ref,
    right_ref,
    block_ref,
    own_ref,
    left_ref,
    edge_ref,
    q1,
    q2,
    q3,
    g1,
    g3,
    g2,
    image_ref,
    stats_ref,
    flips,
    lefts,
    psi,
    values_ref,
    sems,
):
    row = lax.axis_index("row")
    group, spin = place()
    count = left_ref.shape[0]
    sign_one = (1 - 2 * (spin // 2)).astype(F32)
    field_one, field_two = fields_ref[0, 0], fields_ref[0, 1]
    copies = []

    def fetch(source, target):
        copies.append(pltpu.make_async_copy(source, target, sems.at[len(copies)]))

    mine = rows_at(spin, count)
    fetch(left_ref, lefts.at[0, mine, :])
    fetch(edge_ref, lefts.at[1, mine, :])
    for step, ref in ((1, q1), (3, q3), (2, q2)):
        rows = rows_at((spin - step) % SIDE, count)
        fetch(ref.at[2], lefts.at[0, rows, :])
        fetch(ref.at[3], lefts.at[1, rows, :])
    for step, ref in ((0, block_ref), (1, g1), (3, g3), (2, g2)):
        for i in range(SIDE):
            at = row_of((group - step) % SIDE, i)
            fetch(ref.at[i * count : (i + 1) * count, :], psi.at[rows_at(at, count), :])
    psi_here = len(copies)
    fetch(own_ref.at[spin ^ 1], flips.at[0, mine, :])
    fetch(own_ref.at[spin ^ 2], flips.at[1, mine, :])
    for step, ref in ((1, q1), (3, q3), (2, q2)):
        rows = rows_at((spin - step) % SIDE, count)
        fetch(ref.at[0], flips.at[0, rows, :])
        fetch(ref.at[1], flips.at[1, rows, :])
    fetch(block_ref, values_ref)
    for copy in copies:
        copy.start()
    for copy in copies[:psi_here]:
        copy.wait()
    applied = dot(lefts[0], psi[...]) + sign_one * dot(lefts[1], psi[...])
    for copy in copies[psi_here:]:
        copy.wait()
    values = values_ref[...].astype(F32)
    applied = (
        applied
        + right_ref[...]
        - field_one * flips[1].astype(F32)
        - field_two * flips[0].astype(F32)
    )
    squares = jnp.sum(values * values)
    rayleigh = jnp.sum(values * applied)
    quotient = jnp.where(squares > 0.0, rayleigh / squares, 0.0)
    image = applied - quotient * values
    image_ref[...] = image.astype(BF16)
    spread = jnp.sum(image * image)
    cross = jnp.sum(image * values)
    lane = lax.broadcasted_iota(jnp.int32, stats_ref.shape, 1)
    here = lax.broadcasted_iota(jnp.int32, stats_ref.shape, 0) == row
    stats = jnp.zeros(stats_ref.shape, F32)
    for i, item in enumerate((squares, rayleigh, spread, cross, quotient)):
        stats = jnp.where(here & (lane == i), item, stats)
    stats_ref[...] = stats


def gram_kernel(
    s0, s1, s2, s3, b0, a0, b1, a1, b3, a3, b2, a2, wave_ref, energy_ref, own_ref, o0, o1, o2, o3,
    psi, image, total, sems,
):
    group, spin = place()
    count = own_ref.shape[0]
    depth = SIDE * count
    bond = own_ref.shape[1]
    copies = []
    for i, ref in enumerate((b0, a0, b1, a1, b3, a3, b2, a2)):
        target = (psi, image)[i % 2].at[i // 2]
        copies.append(pltpu.make_async_copy(ref, target, sems.at[i]))
    for copy in copies:
        copy.start()
    stats = s0[...] + s1[...] + s2[...] + s3[...]
    squares, rayleigh, spread, cross, quotient = (stats[:, i : i + 1] for i in range(5))
    all_squares = jnp.sum(squares, axis=0, keepdims=True)
    energy = jnp.sum(rayleigh, axis=0, keepdims=True) / all_squares
    shift = quotient - energy
    distance = jnp.sum(spread + 2.0 * shift * cross + shift * shift * squares, axis=0, keepdims=True)
    renorm = all_squares + STEP_SIZE * STEP_SIZE * distance
    scale = jnp.sqrt(bond / renorm)
    energy_ref[...] = jnp.broadcast_to(energy, energy_ref.shape)
    on_psi = scale * (1.0 - STEP_SIZE * shift)
    on_image = -STEP_SIZE * scale
    device = lax.broadcasted_iota(jnp.int32, on_psi.shape, 0)
    for slot, step in enumerate((0, 1, 3, 2)):
        from_group = (group - step) % SIDE
        there = device == row_of(from_group, spin)
        factor = jnp.sum(jnp.where(there, on_psi, 0.0), axis=0, keepdims=True)
        copies[2 * slot].wait()
        copies[2 * slot + 1].wait()
        for i in range(SIDE):
            rows = slice(i * count, (i + 1) * count)
            wave_ref[rows_at(row_of(from_group, i), count), :] = (
                factor * psi[slot, rows, :].astype(F32)
                + on_image * image[slot, rows, :].astype(F32)
            ).astype(BF16)
    for step, out in ((1, o1), (3, o3), (2, o2), (0, o0)):
        at = row_of(group, (spin + step) % SIDE)
        pair = wave_ref[:, rows_at(at // 2, 2 * count)]
        total[...] = lax.dot_general(
            pair, wave_ref[...], (((0,), (0,)), ((), ())), preferred_element_type=F32
        )
        half = total[rows_at(at % 2, count), :]
        if step == 0:
            own_ref[...] = half
            out[...] = wave_ref[rows_at(at, count), :]
        else:
            out[0] = half.astype(BF16)
            out[1] = wave_ref[rows_at(at, count), :]


def weigh_kernel(kept_ref, p0, p1, p2, p3, bond_ref, out_ref):
    row = lax.axis_index("row")
    gram = p0[...] + p1[0].astype(F32) + p2[0].astype(F32) + p3[0].astype(F32)
    count = gram.shape[0]
    lane = lax.broadcasted_iota(jnp.int32, bond_ref.shape, 1)
    inverse = jnp.where(lane < kept_ref[0], 1.0 / bond_ref[...], 0.0)
    at = lax.broadcasted_iota(jnp.int32, gram.shape, 0) + row * count
    same = lax.broadcasted_iota(jnp.int32, gram.shape, 1) == at
    column = jnp.sum(jnp.where(same, inverse, 0.0), axis=1, keepdims=True)
    out_ref[...] = (column * gram * inverse).astype(BF16)


def join_kernel(w0, w1, w2, w3, wave_ref, o0, o1, o2, o3, weights):
    count = w0.shape[0]
    for i, ref in enumerate((w0, w1, w2, w3)):
        weights[i * count : (i + 1) * count, :] = ref[...]
    product = dot(weights[...], wave_ref[...]).astype(BF16)
    for i, out in enumerate((o0, o1, o2, o3)):
        out[...] = product[i * count : (i + 1) * count, :]


def body(
    wavefunction, left_block, left_edge, right_block, right_edge, fields, bond_values, kept_rank
):
    count, _, bond = wavefunction.shape
    depth = SIDE * count
    _, spin = place()
    spins = jnp.moveaxis(wavefunction, 1, 0)

    def rows_of_spin(index):
        return lax.dynamic_index_in_dim(spins, index, 0, keepdims=False)

    early = [along_spin(rows_of_spin((spin + s) % SIDE), s) for s in (1, 2, 3)]
    (block,) = call(assemble_kernel, [shape((depth, bond), BF16)], [spins, *early], 0)
    g1, g3, g2 = (along_group(block, s) for s in (1, 3, 2))

    def bundle(s):
        target = (spin + s) % SIDE
        return jnp.stack(
            [rows_of_spin(target ^ 1), rows_of_spin(target ^ 2), left_block, left_edge]
        )

    q1, q2, q3 = (along_spin(bundle(s), s) for s in (1, 2, 3))
    (right,) = call(
        right_kernel,
        [shape((depth, bond), F32)],
        [block, right_block, right_edge],
        4 * depth * bond * bond,
    )
    image, stats = call(
        left_kernel,
        [shape((depth, bond), BF16), shape((SIDE * SIDE, 128), F32)],
        [fields, right, block, spins, left_block, left_edge, q1, q2, q3, g1, g3, g2],
        4 * depth * bond * bond,
        scratch=[
            pltpu.VMEM((2, depth, bond), BF16),
            pltpu.VMEM((2, depth, bond), BF16),
            pltpu.VMEM((SIDE * depth, bond), BF16),
            pltpu.VMEM((depth, bond), BF16),
            pltpu.SemaphoreType.DMA((4 * 2 + 4 * SIDE + 4 * 2 + 1,)),
        ],
        smem=(0,),
        far=range(2, 12),
    )
    a1, a3, a2 = (along_group(image, s) for s in (1, 3, 2))
    stats = stats + along_spin(stats, 1) + along_spin(stats, 2) + along_spin(stats, 3)
    all_stats = [stats] + [along_group(stats, s) for s in (1, 2, 3)]

    wave, energy, own_gram, own_rows, *packets = call(
        gram_kernel,
        [
            shape((SIDE * depth, bond), BF16),
            shape((8, 128), F32),
            shape((count, bond), F32),
            shape((count, bond), BF16),
        ]
        + [shape((2, count, bond), BF16)] * 3,
        [*all_stats, block, image, g1, a1, g3, a3, g2, a2],
        4 * depth * bond * bond,
        scratch=[
            pltpu.VMEM((SIDE, depth, bond), BF16),
            pltpu.VMEM((SIDE, depth, bond), BF16),
            pltpu.VMEM((2 * count, bond), F32),
            pltpu.SemaphoreType.DMA((2 * SIDE,)),
        ],
        far=range(4, 12),
    )
    arrived = [along_spin(packets[s - 1], s) for s in (1, 2, 3)]
    (weighted,) = call(
        weigh_kernel,
        [shape((count, bond), BF16)],
        [kept_rank, own_gram, *arrived, bond_values],
        0,
        smem=(0,),
    )
    previous = to_next_segment(weighted)
    blocks = [previous] + [along_spin(previous, s) for s in (1, 2, 3)]
    joined = call(
        join_kernel,
        [shape((count, bond), BF16)] * SIDE,
        [*blocks, wave],
        2 * depth * bond * bond,
        scratch=[pltpu.VMEM((depth, bond), BF16)],
    )
    back = [joined[0]] + [along_spin(joined[s], -s) for s in (1, 2, 3)]
    rows = [own_rows, arrived[2][1], arrived[1][1], arrived[0][1]]
    wave_new, joined_wave = (
        jnp.moveaxis(jnp.roll(jnp.stack(pieces), spin, 0), 0, 1) for pieces in (rows, back)
    )
    return (wave_new, joined_wave, energy[0, 0].reshape(1))


def solution(mesh):
    in_specs = (
        P(("seg", "row"), None, None),
        P(("seg", "row"), None),
        P(("seg", "row"), None),
        P("seg", None),
        P("seg", None),
        P("seg", None),
        P("seg", None),
        P("seg"),
    )
    out_specs = (P(("seg", "row"), None, None), P(("seg", "row"), None, None), P("seg"))
    return jax.shard_map(body, mesh=mesh, in_specs=in_specs, out_specs=out_specs, check_vma=False)
```

```python
import jax
import jax.numpy as jnp
from jax import lax
from jax.experimental import pallas as pl
from jax.experimental.pallas import tpu as pltpu
from jax.sharding import PartitionSpec as P

STEP_SIZE = 0.25

SIDE = 4
F32 = jnp.float32
BF16 = jnp.bfloat16


def place():
    row = lax.axis_index("row")
    odd = lax.axis_index("seg") % 2 == 1
    z, y = row // SIDE, row % SIDE
    return jnp.where(odd, y, z), jnp.where(odd, z, y)


def row_of(group, spin):
    odd = lax.axis_index("seg") % 2 == 1
    return jnp.where(odd, spin * SIDE + group, group * SIDE + spin)


def moved(row, step, on_z):
    z, y = row // SIDE, row % SIDE
    return ((z + step) % SIDE) * SIDE + y if on_z else z * SIDE + (y + step) % SIDE


def along(value, step, over_group):
    rows = SIDE * SIDE
    pairs = [
        (k * rows + row, k * rows + moved(row, step, over_group == (k % 2 == 0)))
        for k in range(lax.axis_size("seg"))
        for row in range(rows)
    ]
    return lax.ppermute(value, ("seg", "row"), pairs)


def along_spin(value, step):
    return along(value, step, False)


def along_group(value, step):
    return along(value, step, True)


def to_next_segment(value):
    return lax.ppermute(value, "seg", [(k, k + 1) for k in range(lax.axis_size("seg") - 1)])


def cost(flops, moved):
    return pl.CostEstimate(flops=flops, bytes_accessed=moved, transcendentals=0)


def call(kernel, outs, args, flops, mebibytes, scratch=(), smem=()):
    moved_bytes = sum(a.size * a.dtype.itemsize for a in args)
    moved_bytes += sum(o.size * o.dtype.itemsize for o in outs)

    def space(i):
        return pltpu.SMEM if i in smem else pltpu.VMEM

    return pl.pallas_call(
        kernel,
        out_shape=tuple(outs),
        in_specs=[pl.BlockSpec(memory_space=space(i)) for i in range(len(args))],
        out_specs=tuple(pl.BlockSpec(memory_space=pltpu.VMEM) for _ in outs),
        scratch_shapes=list(scratch),
        cost_estimate=cost(flops, moved_bytes),
        compiler_params=pltpu.CompilerParams(vmem_limit_bytes=mebibytes << 20),
    )(*args)


def shape(dims, dtype):
    return jax.ShapeDtypeStruct(dims, dtype)


def rows_at(index, count):
    return pl.ds(pl.multiple_of(index * count, count), count)


def dot(a, b):
    return jnp.dot(a, b, preferred_element_type=F32)


def assemble_kernel(own_ref, p1, p2, p3, out_ref):
    _, spin = place()
    count = p1.shape[0]
    out_ref[rows_at(spin, count), :] = own_ref[spin]
    for step, ref in ((1, p1), (2, p2), (3, p3)):
        out_ref[rows_at((spin - step) % SIDE, count), :] = ref[...]


def right_kernel(block_ref, rh_ref, rz_ref, out_ref):
    _, spin = place()
    sign_one = (1 - 2 * (spin // 2)).astype(F32)
    sign_two = (1 - 2 * (spin % 2)).astype(F32)
    block = block_ref[...]
    total = dot(block, rh_ref[...]) + sign_two * dot(block, rz_ref[...])
    out_ref[...] = total - (sign_one * sign_two) * block.astype(F32)


def left_kernel(
    fields_ref,
    right_ref,
    block_ref,
    own_ref,
    left_ref,
    edge_ref,
    q1,
    q2,
    q3,
    g1,
    g3,
    g2,
    image_ref,
    stats_ref,
    flips,
    lefts,
    psi,
):
    row = lax.axis_index("row")
    group, spin = place()
    count = left_ref.shape[0]
    sign_one = (1 - 2 * (spin // 2)).astype(F32)
    field_one, field_two = fields_ref[0, 0], fields_ref[0, 1]

    def put(at, flip_two, flip_one, left, edge):
        rows = rows_at(at, count)
        lefts[0, rows, :] = left
        lefts[1, rows, :] = edge
        flips[rows, :] = (
            right_ref[rows, :] - field_one * flip_one.astype(F32) - field_two * flip_two.astype(F32)
        )

    put(spin, own_ref[spin ^ 1], own_ref[spin ^ 2], left_ref[...], edge_ref[...])
    for step, ref in ((1, q1), (2, q2), (3, q3)):
        put((spin - step) % SIDE, ref[0], ref[1], ref[2], ref[3])
    for step, ref in ((0, block_ref), (1, g1), (3, g3), (2, g2)):
        for i in range(SIDE):
            at = row_of((group - step) % SIDE, i)
            psi[rows_at(at, count), :] = ref[i * count : (i + 1) * count, :]
    applied = flips[...] + dot(lefts[0], psi[...]) + sign_one * dot(lefts[1], psi[...])
    values = block_ref[...].astype(F32)
    squares = jnp.sum(values * values)
    rayleigh = jnp.sum(values * applied)
    quotient = jnp.where(squares > 0.0, rayleigh / squares, 0.0)
    image = applied - quotient * values
    image_ref[...] = image.astype(BF16)
    spread = jnp.sum(image * image)
    cross = jnp.sum(image * values)
    lane = lax.broadcasted_iota(jnp.int32, stats_ref.shape, 1)
    here = lax.broadcasted_iota(jnp.int32, stats_ref.shape, 0) == row
    stats = jnp.zeros(stats_ref.shape, F32)
    for i, item in enumerate((squares, rayleigh, spread, cross, quotient)):
        stats = jnp.where(here & (lane == i), item, stats)
    stats_ref[...] = stats


def gram_kernel(
    s0, s1, s2, s3, b0, a0, b1, a1, b3, a3, b2, a2, wave_ref, energy_ref, own_ref, o0, o1, o2, o3,
    total,
):
    group, spin = place()
    count = own_ref.shape[0]
    bond = own_ref.shape[1]
    stats = s0[...] + s1[...] + s2[...] + s3[...]
    squares, rayleigh, spread, cross, quotient = (stats[:, i : i + 1] for i in range(5))
    all_squares = jnp.sum(squares, axis=0, keepdims=True)
    energy = jnp.sum(rayleigh, axis=0, keepdims=True) / all_squares
    shift = quotient - energy
    distance = jnp.sum(spread + 2.0 * shift * cross + shift * shift * squares, axis=0, keepdims=True)
    renorm = all_squares + STEP_SIZE * STEP_SIZE * distance
    scale = jnp.sqrt(bond / renorm)
    energy_ref[...] = jnp.broadcast_to(energy, energy_ref.shape)
    on_psi = scale * (1.0 - STEP_SIZE * shift)
    on_image = -STEP_SIZE * scale
    device = lax.broadcasted_iota(jnp.int32, on_psi.shape, 0)
    for step, psi, image in ((0, b0, a0), (1, b1, a1), (3, b3, a3), (2, b2, a2)):
        from_group = (group - step) % SIDE
        there = device == row_of(from_group, spin)
        factor = jnp.sum(jnp.where(there, on_psi, 0.0), axis=0, keepdims=True)
        for i in range(SIDE):
            rows = slice(i * count, (i + 1) * count)
            wave_ref[rows_at(row_of(from_group, i), count), :] = (
                factor * psi[rows, :].astype(F32) + on_image * image[rows, :].astype(F32)
            ).astype(BF16)
    for step, out in ((1, o1), (3, o3), (2, o2), (0, o0)):
        at = row_of(group, (spin + step) % SIDE)
        pair = wave_ref[:, rows_at(at // 2, 2 * count)]
        total[...] = lax.dot_general(
            pair, wave_ref[...], (((0,), (0,)), ((), ())), preferred_element_type=F32
        )
        half = total[rows_at(at % 2, count), :]
        if step == 0:
            own_ref[...] = half
            out[...] = wave_ref[rows_at(at, count), :]
        else:
            out[0] = half.astype(BF16)
            out[1] = wave_ref[rows_at(at, count), :]


def weigh_kernel(kept_ref, p0, p1, p2, p3, bond_ref, out_ref):
    row = lax.axis_index("row")
    gram = p0[...] + p1[0].astype(F32) + p2[0].astype(F32) + p3[0].astype(F32)
    count = gram.shape[0]
    lane = lax.broadcasted_iota(jnp.int32, bond_ref.shape, 1)
    inverse = jnp.where(lane < kept_ref[0], 1.0 / bond_ref[...], 0.0)
    at = lax.broadcasted_iota(jnp.int32, gram.shape, 0) + row * count
    same = lax.broadcasted_iota(jnp.int32, gram.shape, 1) == at
    column = jnp.sum(jnp.where(same, inverse, 0.0), axis=1, keepdims=True)
    out_ref[...] = (column * gram * inverse).astype(BF16)


def join_kernel(w0, w1, w2, w3, wave_ref, o0, o1, o2, o3, weights):
    count = w0.shape[0]
    for i, ref in enumerate((w0, w1, w2, w3)):
        weights[i * count : (i + 1) * count, :] = ref[...]
    product = dot(weights[...], wave_ref[...]).astype(BF16)
    for i, out in enumerate((o0, o1, o2, o3)):
        out[...] = product[i * count : (i + 1) * count, :]


def body(
    wavefunction, left_block, left_edge, right_block, right_edge, fields, bond_values, kept_rank
):
    count, _, bond = wavefunction.shape
    depth = SIDE * count
    _, spin = place()
    spins = jnp.moveaxis(wavefunction, 1, 0)

    def rows_of_spin(index):
        return lax.dynamic_index_in_dim(spins, index, 0, keepdims=False)

    early = [along_spin(rows_of_spin((spin + s) % SIDE), s) for s in (1, 2, 3)]
    (block,) = call(assemble_kernel, [shape((depth, bond), BF16)], [spins, *early], 0, 4)
    g1, g3, g2 = (along_group(block, s) for s in (1, 3, 2))

    def bundle(s):
        target = (spin + s) % SIDE
        return jnp.stack(
            [rows_of_spin(target ^ 1), rows_of_spin(target ^ 2), left_block, left_edge]
        )

    q1, q2, q3 = (along_spin(bundle(s), s) for s in (1, 2, 3))
    (right,) = call(
        right_kernel,
        [shape((depth, bond), F32)],
        [block, right_block, right_edge],
        4 * depth * bond * bond,
        12,
    )
    image, stats = call(
        left_kernel,
        [shape((depth, bond), BF16), shape((SIDE * SIDE, 128), F32)],
        [fields, right, block, spins, left_block, left_edge, q1, q2, q3, g1, g3, g2],
        4 * depth * bond * bond,
        12,
        scratch=[
            pltpu.VMEM((depth, bond), F32),
            pltpu.VMEM((2, depth, bond), BF16),
            pltpu.VMEM((SIDE * depth, bond), BF16),
        ],
        smem=(0,),
    )
    a1, a3, a2 = (along_group(image, s) for s in (1, 3, 2))
    stats = stats + along_spin(stats, 1) + along_spin(stats, 2) + along_spin(stats, 3)
    all_stats = [stats] + [along_group(stats, s) for s in (1, 2, 3)]

    wave, energy, own_gram, own_rows, *packets = call(
        gram_kernel,
        [
            shape((SIDE * depth, bond), BF16),
            shape((8, 128), F32),
            shape((count, bond), F32),
            shape((count, bond), BF16),
        ]
        + [shape((2, count, bond), BF16)] * 3,
        [*all_stats, block, image, g1, a1, g3, a3, g2, a2],
        4 * depth * bond * bond,
        12,
        scratch=[pltpu.VMEM((2 * count, bond), F32)],
    )
    arrived = [along_spin(packets[s - 1], s) for s in (1, 2, 3)]
    (weighted,) = call(
        weigh_kernel,
        [shape((count, bond), BF16)],
        [kept_rank, own_gram, *arrived, bond_values],
        0,
        6,
        smem=(0,),
    )
    previous = to_next_segment(weighted)
    blocks = [previous] + [along_spin(previous, s) for s in (1, 2, 3)]
    joined = call(
        join_kernel,
        [shape((count, bond), BF16)] * SIDE,
        [*blocks, wave],
        2 * depth * bond * bond,
        8,
        scratch=[pltpu.VMEM((depth, bond), BF16)],
    )
    back = [joined[0]] + [along_spin(joined[s], -s) for s in (1, 2, 3)]
    rows = [own_rows, arrived[2][1], arrived[1][1], arrived[0][1]]
    wave_new, joined_wave = (
        jnp.moveaxis(jnp.roll(jnp.stack(pieces), spin, 0), 0, 1) for pieces in (rows, back)
    )
    return (wave_new, joined_wave, energy[0, 0].reshape(1))


def solution(mesh):
    in_specs = (
        P(("seg", "row"), None, None),
        P(("seg", "row"), None),
        P(("seg", "row"), None),
        P("seg", None),
        P("seg", None),
        P("seg", None),
        P("seg", None),
        P("seg"),
    )
    out_specs = (P(("seg", "row"), None, None), P(("seg", "row"), None, None), P("seg"))
    return jax.shard_map(body, mesh=mesh, in_specs=in_specs, out_specs=out_specs, check_vma=False)
```

```python
import jax
import jax.numpy as jnp
from jax import lax
from jax.experimental import pallas as pl
from jax.experimental.pallas import tpu as pltpu
from jax.sharding import PartitionSpec as P

STEP_SIZE = 0.25

SIDE = 4
F32 = jnp.float32
BF16 = jnp.bfloat16


def place():
    row = lax.axis_index("row")
    odd = lax.axis_index("seg") % 2 == 1
    z, y = row // SIDE, row % SIDE
    return jnp.where(odd, y, z), jnp.where(odd, z, y)


def row_of(group, spin):
    odd = lax.axis_index("seg") % 2 == 1
    return jnp.where(odd, spin * SIDE + group, group * SIDE + spin)


def moved(row, step, on_z):
    z, y = row // SIDE, row % SIDE
    return ((z + step) % SIDE) * SIDE + y if on_z else z * SIDE + (y + step) % SIDE


def along(value, step, over_group):
    rows = SIDE * SIDE
    pairs = [
        (k * rows + row, k * rows + moved(row, step, over_group == (k % 2 == 0)))
        for k in range(lax.axis_size("seg"))
        for row in range(rows)
    ]
    return lax.ppermute(value, ("seg", "row"), pairs)


def along_spin(value, step):
    return along(value, step, False)


def along_group(value, step):
    return along(value, step, True)


def to_next_segment(value):
    return lax.ppermute(value, "seg", [(k, k + 1) for k in range(lax.axis_size("seg") - 1)])


def cost(flops, moved):
    return pl.CostEstimate(flops=flops, bytes_accessed=moved, transcendentals=0)


def call(kernel, outs, args, flops, mebibytes, scratch=(), smem=()):
    moved_bytes = sum(a.size * a.dtype.itemsize for a in args)
    moved_bytes += sum(o.size * o.dtype.itemsize for o in outs)

    def space(i):
        return pltpu.SMEM if i in smem else pltpu.VMEM

    return pl.pallas_call(
        kernel,
        out_shape=tuple(outs),
        in_specs=[pl.BlockSpec(memory_space=space(i)) for i in range(len(args))],
        out_specs=tuple(pl.BlockSpec(memory_space=pltpu.VMEM) for _ in outs),
        scratch_shapes=list(scratch),
        cost_estimate=cost(flops, moved_bytes),
        compiler_params=pltpu.CompilerParams(vmem_limit_bytes=mebibytes << 20),
    )(*args)


def shape(dims, dtype):
    return jax.ShapeDtypeStruct(dims, dtype)


def rows_at(index, count):
    return pl.ds(pl.multiple_of(index * count, count), count)


def dot(a, b):
    return jnp.dot(a, b, preferred_element_type=F32)


def assemble_kernel(own_ref, p1, p2, p3, out_ref):
    _, spin = place()
    count = p1.shape[0]
    out_ref[rows_at(spin, count), :] = own_ref[spin]
    for step, ref in ((1, p1), (2, p2), (3, p3)):
        out_ref[rows_at((spin - step) % SIDE, count), :] = ref[...]


def right_kernel(block_ref, rh_ref, rz_ref, out_ref):
    _, spin = place()
    sign_one = (1 - 2 * (spin // 2)).astype(F32)
    sign_two = (1 - 2 * (spin % 2)).astype(F32)
    block = block_ref[...]
    total = dot(block, rh_ref[...]) + sign_two * dot(block, rz_ref[...])
    out_ref[...] = total - (sign_one * sign_two) * block.astype(F32)


def near_kernel(
    fields_ref,
    right_ref,
    block_ref,
    own_ref,
    left_ref,
    edge_ref,
    q1,
    q2,
    q3,
    g1,
    g3,
    part_ref,
    far_ref,
    lefts,
):
    group, spin = place()
    odd = lax.axis_index("seg") % 2 == 1
    count = left_ref.shape[0]
    depth = block_ref.shape[0]
    wide = 2 * count
    sign_one = (1 - 2 * (spin // 2)).astype(F32)
    field_one, field_two = fields_ref[0, 0], fields_ref[0, 1]
    low = lax.broadcasted_iota(jnp.int32, (count, wide), 1) < count

    def columns_by_group(source, rows, which, sign):
        for g in range(SIDE):
            for p in range(SIDE // 2):
                straight = source[:, (g * SIDE + 2 * p) * count :][:, :wide].astype(F32)
                first, second = ((SIDE * i + g) // 2 * wide for i in (2 * p, 2 * p + 1))
                a = source[:, first : first + wide].astype(F32)
                b = source[:, second : second + wide].astype(F32)
                if g % 2:
                    a = pltpu.roll(a, count, 1)
                else:
                    b = pltpu.roll(b, count, 1)
                ordered = jnp.where(odd, jnp.where(low, a, b), straight)
                at = g * depth + p * wide
                lefts[which, rows, at : at + wide] = (sign * ordered).astype(BF16)

    def put(at, flips, left, edge):
        rows = rows_at(at, count)
        part_ref[rows, :] = right_ref[rows, :] - flips
        columns_by_group(left, rows, 0, 1.0)
        columns_by_group(edge, rows, 1, sign_one)

    flips = field_one * own_ref[spin ^ 2].astype(F32) + field_two * own_ref[spin ^ 1].astype(F32)
    put(spin, flips, left_ref[...], edge_ref[...])
    for step, ref in ((1, q1), (2, q2), (3, q3)):
        put((spin - step) % SIDE, ref[0].astype(F32), ref[1], ref[2])
    part = part_ref[...]
    for step, ref in ((0, block_ref), (1, g1), (3, g3)):
        columns = rows_at((group - step) % SIDE, depth)
        block = ref[...]
        part += dot(lefts[0, :, columns], block) + dot(lefts[1, :, columns], block)
    part_ref[...] = part
    columns = rows_at((group - 2) % SIDE, depth)
    far_ref[0] = lefts[0, :, columns]
    far_ref[1] = lefts[1, :, columns]


def far_kernel(part_ref, far_ref, block_ref, g2, image_ref, stats_ref):
    row = lax.axis_index("row")
    block = g2[...]
    applied = part_ref[...] + dot(far_ref[0], block) + dot(far_ref[1], block)
    values = block_ref[...].astype(F32)
    squares = jnp.sum(values * values)
    rayleigh = jnp.sum(values * applied)
    quotient = jnp.where(squares > 0.0, rayleigh / squares, 0.0)
    image = applied - quotient * values
    image_ref[...] = image.astype(BF16)
    spread = jnp.sum(image * image)
    cross = jnp.sum(image * values)
    lane = lax.broadcasted_iota(jnp.int32, stats_ref.shape, 1)
    here = lax.broadcasted_iota(jnp.int32, stats_ref.shape, 0) == row
    stats = jnp.zeros(stats_ref.shape, F32)
    for i, item in enumerate((squares, rayleigh, spread, cross, quotient)):
        stats = jnp.where(here & (lane == i), item, stats)
    stats_ref[...] = stats


def gram_kernel(
    s0, s1, s2, s3, b0, a0, b1, a1, b3, a3, b2, a2, wave_ref, energy_ref, o0, o1, o2, o3,
    r0, r1, r2, r3, total,
):
    group, spin = place()
    count, bond = o0.shape
    stats = s0[...] + s1[...] + s2[...] + s3[...]
    squares, rayleigh, spread, cross, quotient = (stats[:, i : i + 1] for i in range(5))
    all_squares = jnp.sum(squares, axis=0, keepdims=True)
    energy = jnp.sum(rayleigh, axis=0, keepdims=True) / all_squares
    shift = quotient - energy
    distance = jnp.sum(spread + 2.0 * shift * cross + shift * shift * squares, axis=0, keepdims=True)
    renorm = all_squares + STEP_SIZE * STEP_SIZE * distance
    scale = jnp.sqrt(bond / renorm)
    energy_ref[...] = jnp.broadcast_to(energy, energy_ref.shape)
    on_psi = scale * (1.0 - STEP_SIZE * shift)
    on_image = -STEP_SIZE * scale
    device = lax.broadcasted_iota(jnp.int32, on_psi.shape, 0)
    for step, psi, image in ((0, b0, a0), (1, b1, a1), (3, b3, a3), (2, b2, a2)):
        from_group = (group - step) % SIDE
        there = device == row_of(from_group, spin)
        factor = jnp.sum(jnp.where(there, on_psi, 0.0), axis=0, keepdims=True)
        for i in range(SIDE):
            rows = slice(i * count, (i + 1) * count)
            wave_ref[rows_at(row_of(from_group, i), count), :] = (
                factor * psi[rows, :].astype(F32) + on_image * image[rows, :].astype(F32)
            ).astype(BF16)
    for step, out, rows_ref in ((1, o1, r1), (3, o3, r3), (2, o2, r2), (0, o0, r0)):
        at = row_of(group, (spin + step) % SIDE)
        pair = wave_ref[:, rows_at(at // 2, 2 * count)]
        total[...] = lax.dot_general(
            pair, wave_ref[...], (((0,), (0,)), ((), ())), preferred_element_type=F32
        )
        out[...] = total[rows_at(at % 2, count), :].astype(out.dtype)
        rows_ref[...] = wave_ref[rows_at(at, count), :]


def weigh_kernel(kept_ref, p0, p1, p2, p3, bond_ref, out_ref):
    row = lax.axis_index("row")
    gram = p0[...] + p1[...].astype(F32) + p2[...].astype(F32) + p3[...].astype(F32)
    count = gram.shape[0]
    lane = lax.broadcasted_iota(jnp.int32, bond_ref.shape, 1)
    inverse = jnp.where(lane < kept_ref[0], 1.0 / bond_ref[...], 0.0)
    at = lax.broadcasted_iota(jnp.int32, gram.shape, 0) + row * count
    same = lax.broadcasted_iota(jnp.int32, gram.shape, 1) == at
    column = jnp.sum(jnp.where(same, inverse, 0.0), axis=1, keepdims=True)
    out_ref[...] = (column * gram * inverse).astype(BF16)


def join_kernel(*refs):
    many = (len(refs) - 1) // 2
    count = refs[0].shape[0]
    weights = jnp.concatenate([ref[...] for ref in refs[:many]])
    product = dot(weights, refs[many][...]).astype(BF16)
    for i, out in enumerate(refs[many + 1 :]):
        out[...] = product[i * count : (i + 1) * count, :]


def body(
    wavefunction, left_block, left_edge, right_block, right_edge, fields, bond_values, kept_rank
):
    count, _, bond = wavefunction.shape
    depth = SIDE * count
    _, spin = place()
    spins = jnp.moveaxis(wavefunction, 1, 0)

    def rows_of_spin(index):
        return lax.dynamic_index_in_dim(spins, index, 0, keepdims=False)

    early = [along_spin(rows_of_spin((spin + s) % SIDE), s) for s in (1, 2, 3)]
    (block,) = call(assemble_kernel, [shape((depth, bond), BF16)], [spins, *early], 0, 4)
    g1, g3, g2 = (along_group(block, s) for s in (1, 3, 2))

    def bundle(s):
        target = (spin + s) % SIDE
        flips = fields[0, 0] * rows_of_spin(target ^ 2) + fields[0, 1] * rows_of_spin(target ^ 1)
        return jnp.stack([flips.astype(BF16), left_block, left_edge])

    q1, q2, q3 = (along_spin(bundle(s), s) for s in (1, 2, 3))
    (right,) = call(
        right_kernel,
        [shape((depth, bond), F32)],
        [block, right_block, right_edge],
        4 * depth * bond * bond,
        12,
    )
    part, far = call(
        near_kernel,
        [shape((depth, bond), F32), shape((2, depth, depth), BF16)],
        [fields, right, block, spins, left_block, left_edge, q1, q2, q3, g1, g3],
        3 * depth * bond * bond,
        12,
        scratch=[pltpu.VMEM((2, depth, bond), BF16)],
        smem=(0,),
    )
    image, stats = call(
        far_kernel,
        [shape((depth, bond), BF16), shape((SIDE * SIDE, 128), F32)],
        [part, far, block, g2],
        depth * bond * bond,
        12,
    )
    a1, a3, a2 = (along_group(image, s) for s in (1, 3, 2))
    stats = stats + along_spin(stats, 1) + along_spin(stats, 2) + along_spin(stats, 3)
    all_stats = [stats] + [along_group(stats, s) for s in (1, 2, 3)]

    wave, energy, g0, *rest = call(
        gram_kernel,
        [shape((SIDE * depth, bond), BF16), shape((8, 128), F32), shape((count, bond), F32)]
        + [shape((count, bond), BF16)] * (2 * SIDE - 1),
        [*all_stats, block, image, g1, a1, g3, a3, g2, a2],
        4 * depth * bond * bond,
        12,
        scratch=[pltpu.VMEM((2 * count, bond), F32)],
    )
    partial, rows = rest[: SIDE - 1], rest[SIDE - 1 :]
    partials = [g0]
    for s in (1, 2, 3):
        partials.append(along_spin(partial[s - 1], s))
    pieces = [rows[0]]
    for s in (1, 2, 3):
        pieces.append(along_spin(rows[s], s))
    (weighted,) = call(
        weigh_kernel,
        [shape((count, bond), BF16)],
        [kept_rank, *partials, bond_values],
        0,
        6,
        smem=(0,),
    )
    previous = to_next_segment(weighted)
    w1, w3, w2 = (along_spin(previous, s) for s in (1, 3, 2))
    j0, j1, j3 = call(
        join_kernel,
        [shape((count, bond), BF16)] * 3,
        [previous, w1, w3, wave],
        2 * 3 * count * bond * bond,
        8,
    )
    (j2,) = call(
        join_kernel, [shape((count, bond), BF16)], [w2, wave], 2 * count * bond * bond, 8
    )
    back = [j0] + [along_spin(j, -s) for s, j in ((1, j1), (2, j2), (3, j3))]
    pieces = [pieces[0], pieces[3], pieces[2], pieces[1]]
    wave_new, joined_wave = (
        jnp.moveaxis(jnp.roll(jnp.stack(parts), spin, 0), 0, 1) for parts in (pieces, back)
    )
    return (wave_new, joined_wave, energy[0, 0].reshape(1))


def solution(mesh):
    in_specs = (
        P(("seg", "row"), None, None),
        P(("seg", "row"), None),
        P(("seg", "row"), None),
        P("seg", None),
        P("seg", None),
        P("seg", None),
        P("seg", None),
        P("seg"),
    )
    out_specs = (P(("seg", "row"), None, None), P(("seg", "row"), None, None), P("seg"))
    return jax.shard_map(body, mesh=mesh, in_specs=in_specs, out_specs=out_specs, check_vma=False)
```
